256 devices in a mesh: freq: 8 (over y, core), apt: 8 (over z), rcv: 4 (over x).
Axes of the slice: x: 4, y: 4, z: 8, core: 2. Of those that a mesh axis runs over, the one named last changes fastest.
Arguments:
- shot_lists: bfloat16 [256, 128, 8, 2, 128], P(('apt', 'rcv', 'freq')), may hold values from -6 to 6
- block_ids: int32 [256, 8], P(('apt', 'rcv')), may hold values from 0 to 15, all different within a row
- taper_ids: int32 [256, 8], P(('apt', 'rcv')), may hold values from 0 to 3
- green_traces: bfloat16 [128, 2, 2048, 2048], P('freq', None, 'apt', 'rcv'), may hold values from -0.1875 to 0.1875
Outputs:
- prediction: bfloat16 [256, 128, 2, 2048], P('apt', 'freq', None, 'rcv')
The draws below stay inside these ranges and needn't reach their ends.
Inputs may be any that keep to these rules, and one draw needn't show every extreme that they name: `block_ids`: each output shot names 8 different aperture blocks, and every block is named by some shot.
All inputs are finite; a program needn't handle non-finite values.
Results may differ from the reference program's by a relative error of at most 0.015.
Values may be sent and summed in bfloat16 or wider, within the bound.
A program may use at most 128 MiB of HBM per device.

```python
import jax
import jax.numpy as jnp
from jax import lax

R = 2048
KB = 16
BLK = 128
NB = 8
NF = 128
S = 256
N_APT = 8


def place_ends(values, stream_key, low, top_value):
    shape = values.shape
    spot = [jax.random.randint(jax.random.fold_in(stream_key, axis), (), 0, shape[axis]) for axis in range(len(shape))]
    values = values.at[tuple(spot)].set(low)
    longest = shape.index(max(shape))
    spot[longest] = (spot[longest] + 1) % shape[longest]
    return values.at[tuple(spot)].set(top_value)


def level_of(rng, shape, cuts, low, largest):
    loudness, own = 1.0, jax.random.fold_in(rng, 6)
    for axis_at, parts in cuts:
        draws = jnp.exp(jax.random.uniform(jax.random.fold_in(own, axis_at), (parts,), jnp.float32, low / len(cuts), largest / len(cuts)))
        loudness = loudness * jnp.repeat(draws, shape[axis_at] // parts).reshape([-1 if axis == axis_at else 1 for axis in range(len(shape))])
    return loudness


def choose_distinct(key, rows, number_of, top, lift):
    order = jax.random.permutation(jax.random.fold_in(key, 1), number_of)
    favour = order
    for power in range(3):
        favour = favour * favour // number_of
    favour = favour * lift // number_of
    tickets = jax.random.randint(jax.random.fold_in(key, 2), (rows, number_of), 0, 4096) + favour
    fixed_rows = jax.random.permutation(jax.random.fold_in(key, 3), rows)[jnp.arange(number_of) % rows]
    tickets = jnp.where(jnp.arange(rows)[:, None] == fixed_rows[None, :], 1 << 14, tickets)
    merit = tickets * number_of + jnp.arange(number_of)
    return lax.top_k(merit.astype(jnp.int32), top)[1].astype(jnp.int32)


def gaussian(key, extent, spread, reach, cuts=(), kind=jnp.bfloat16):
    values = jax.random.normal(key, extent, jnp.float32) * spread
    if len(cuts) > 0:
        values = level_of(key, extent, cuts, -0.22, 0.18) * values
    return jnp.clip(values, min=-reach, max=reach).astype(kind)


def setup_inputs(seed: int = 0) -> dict:
    key_list = jax.random.split(jax.random.key(seed), 5)
    return {
        "shot_lists": gaussian(key_list[0], (S, NF, NB, 2, BLK), 1.0, 6.0, ((0, 256),)),
        "block_ids": choose_distinct(key_list[1], S, KB, NB, 8192),
        "taper_ids": place_ends(jax.random.randint(key_list[2], (S, NB), 0, 4), jax.random.fold_in(key_list[2], 1), 0, 3).astype(jnp.int32),
        "green_traces": gaussian(key_list[3], (NF, 2, KB * BLK, R), (NB * BLK) ** -0.5, 0.1875, ((0, 8), (2, 8), (3, 4))),
    }


def windows(block_len):
    angles = jnp.pi * (jnp.arange(block_len, dtype=jnp.float32) + 0.5) / block_len
    cosine = jnp.cos(angles)
    return jnp.stack([jnp.ones_like(cosine), 0.5 - 0.5 * cosine, 0.5 + 0.5 * cosine, jnp.sin(angles) ** 2], axis=0)


def reference(shot_lists, block_ids, taper_ids, green_traces):
    window_rows = windows(BLK)
    taper_rows = window_rows[taper_ids]
    tapered = (shot_lists.astype(jnp.float32) * taper_rows[:, None, :, None, :]).astype(jnp.bfloat16)
    shot_index = jnp.arange(S, dtype=jnp.int32)[:, None]
    group_len = KB * BLK // N_APT

    def one_freq(freq_pos):
        freq_lists = lax.dynamic_index_in_dim(tapered, freq_pos, 1, keepdims=False)
        dense_freq = jnp.zeros((S, KB, 2, BLK), tapered.dtype).at[shot_index, block_ids].set(freq_lists)
        dense_freq = dense_freq.transpose(0, 2, 1, 3).reshape(S, 2, N_APT, group_len).astype(jnp.float32)
        green_freq = lax.dynamic_index_in_dim(green_traces, freq_pos, 0, keepdims=False)
        green_freq = green_freq.astype(jnp.float32).reshape(2, N_APT, group_len, R)
        hp = lax.Precision.HIGHEST
        real_sum = jnp.einsum("sgk,gkr->gsr", dense_freq[:, 0], green_freq[0], precision=hp) - jnp.einsum("sgk,gkr->gsr", dense_freq[:, 1], green_freq[1], precision=hp)
        imag_sum = jnp.einsum("sgk,gkr->gsr", dense_freq[:, 0], green_freq[1], precision=hp) + jnp.einsum("sgk,gkr->gsr", dense_freq[:, 1], green_freq[0], precision=hp)
        group_sums = jnp.stack([real_sum, imag_sum], axis=2)
        group_sums = lax.optimization_barrier(group_sums.astype(jnp.bfloat16)).astype(jnp.float32)
        return jnp.sum(group_sums, axis=0).astype(jnp.bfloat16)

    result = lax.map(one_freq, jnp.arange(NF, dtype=jnp.int32))
    return result.transpose(1, 0, 2, 3)
```

```python
import functools

import jax
import jax.numpy as jnp
from jax import lax
from jax.experimental import pallas as pl
from jax.experimental.pallas import tpu as pltpu
from jax.sharding import PartitionSpec as P

MESH = pl.DeviceIdType.MESH
CHUNKS = 4
SKEW = 4
EARLY = 3


def windows(block_len):
    angles = jnp.pi * (jnp.arange(block_len, dtype=jnp.float32) + 0.5) / block_len
    cosine = jnp.cos(angles)
    return jnp.stack(
        [jnp.ones_like(cosine), 0.5 - 0.5 * cosine, 0.5 + 0.5 * cosine, jnp.sin(angles) ** 2],
        axis=0,
    )


def kernel(
    sizes,
    lists,
    taper,
    select,
    green,
    out,
    raw,
    dense,
    apert,
    held_green,
    partial,
    ring,
    green_sem,
    y_send,
    y_recv,
    z_send,
    z_recv,
    x_send,
    x_recv,
    own_sem,
    ring_send,
    ring_recv,
):
    n_freq, n_apt, n_rcv = sizes
    me_f, me_z, me_x = lax.axis_index("freq"), lax.axis_index("apt"), lax.axis_index("rcv")
    freqs = held_green.shape[0]
    per = freqs // CHUNKS
    steps = n_apt

    barrier = pltpu.get_barrier_semaphore()

    def greet(axis, me, size):
        @pl.loop(1, size)
        def _(off):
            pl.semaphore_signal(
                barrier, inc=1, device_id={axis: lax.rem(me + off, size)}, device_id_type=MESH
            )

    def green_copy(f):
        return pltpu.make_async_copy(green.at[f], held_green.at[f], green_sem.at[f])

    greet("freq", me_f, n_freq)
    greet("apt", me_z, n_apt)
    greet("rcv", me_x, n_rcv)

    def own_lists(c):
        return pltpu.make_async_copy(
            lists.at[pl.ds(me_f * freqs + c * per, per)],
            raw.at[me_f, pl.ds(c * per, per)],
            own_sem.at[0, c],
        )

    @pl.loop(0, CHUNKS)
    def _(c):
        own_lists(c).start()

    pl.semaphore_wait(barrier, n_freq + n_apt + n_rcv - 3)

    def y_copy(c, off):
        peer = lax.rem(me_f + off, n_freq)
        return pltpu.make_async_remote_copy(
            src_ref=lists.at[pl.ds(peer * freqs + c * per, per)],
            dst_ref=raw.at[me_f, pl.ds(c * per, per)],
            send_sem=y_send.at[c, off],
            recv_sem=y_recv.at[c, off],
            device_id={"freq": peer},
            device_id_type=MESH,
        )

    def z_copy(c, off):
        peer = lax.rem(me_z + off, n_apt)
        return pltpu.make_async_remote_copy(
            src_ref=dense.at[pl.ds(c * per, per), peer],
            dst_ref=apert.at[pl.ds(c * per, per), me_z, me_x],
            send_sem=z_send.at[c, off],
            recv_sem=z_recv.at[c, off],
            device_id={"apt": peer},
            device_id_type=MESH,
        )

    def own_dense(c):
        return pltpu.make_async_copy(
            dense.at[pl.ds(c * per, per), me_z],
            apert.at[pl.ds(c * per, per), me_z, me_x],
            own_sem.at[1, c],
        )

    def x_copy(c, off):
        peer = lax.rem(me_x + off, n_rcv)
        mine = apert.at[pl.ds(c * per, per), :, me_x]
        return pltpu.make_async_remote_copy(
            src_ref=mine,
            dst_ref=mine,
            send_sem=x_send.at[c, off],
            recv_sem=x_recv.at[c, off],
            device_id={"rcv": peer},
            device_id_type=MESH,
        )

    def ring_copy(f, t, way):
        goal = lax.rem(me_z - way * (1 + t) + 2 * n_apt, n_apt)
        return pltpu.make_async_remote_copy(
            src_ref=partial.at[f, goal],
            dst_ref=ring.at[f, t],
            send_sem=ring_send.at[f, t],
            recv_sem=ring_recv.at[f, t],
            device_id={"apt": lax.rem(me_z + way + n_apt, n_apt)},
            device_id_type=MESH,
        )

    @pl.loop(0, CHUNKS)
    def _(c):
        @pl.loop(1, n_freq)
        def _(off):
            y_copy(c, off).start()

    @pl.loop(0, freqs)
    def _(f):
        green_copy(f).start()

    @pl.loop(0, CHUNKS)
    def _(c):
        own_lists(c).wait()

        @pl.loop(1, n_freq)
        def _(off):
            y_copy(c, off).wait_recv()

        @pl.loop(0, per)
        def _(i):
            f = c * per + i
            rows = raw[:, f]
            rows = rows.reshape(taper.shape).astype(jnp.float32) * taper[...]
            placed = jnp.dot(
                select[...], rows.astype(jnp.bfloat16), preferred_element_type=jnp.float32
            )
            dense[f] = placed.astype(jnp.bfloat16).reshape(dense.shape[1:])

        own_dense(c).start()

        @pl.loop(1, n_apt)
        def _(off):
            z_copy(c, off).start()

    def spread(c):
        own_dense(c).wait()

        @pl.loop(1, n_apt)
        def _(off):
            z_copy(c, off).wait_recv()

        @pl.loop(1, n_rcv)
        def _(off):
            x_copy(c, off).start()

    @pl.loop(0, EARLY)
    def _(c):
        spread(c)

    def multiply(f):
        green_copy(f).wait()
        blocks = apert.shape[3]
        depth = apert.shape[5]
        rows = apert.shape[1] * apert.shape[2] * apert.shape[4]
        left = jnp.concatenate([apert[f, :, :, b].reshape(rows, depth) for b in range(blocks)], axis=1)
        wide = left.astype(jnp.float32).reshape(rows // 8, 8, blocks * depth)
        odd = lax.rem(lax.broadcasted_iota(jnp.int32, wide.shape, 1), 2) == 1
        turned = jnp.where(odd, pltpu.roll(wide, 1, 1), -pltpu.roll(wide, 7, 1))
        turned = turned.reshape(rows, blocks * depth).astype(jnp.bfloat16)
        both = jnp.concatenate([left, turned], axis=1)
        right = held_green[f].reshape(2 * held_green.shape[2], held_green.shape[3])
        sums = jnp.dot(both, right, preferred_element_type=jnp.float32)
        partial[f] = sums.astype(jnp.bfloat16).reshape(partial.shape[1:])

    def advance(f, t, way):
        goal = lax.rem(me_z - way * (1 + t) + 2 * n_apt, n_apt)
        ring_copy(f, t - 1, way).wait_recv()
        return goal, (
            ring[f, t - 1].astype(jnp.float32) + partial[f, goal].astype(jnp.float32)
        ).astype(jnp.bfloat16)

    @pl.loop(0, steps + SKEW * (CHUNKS - 1))
    def _(tick):
        @pl.loop(0, CHUNKS)
        def _(c):
            t = tick - SKEW * c

            @pl.when(t == 0)
            def _():
                @pl.loop(1, n_rcv)
                def _(off):
                    x_copy(c, off).wait_recv()

                @pl.loop(0, per // 2)
                def _(i):
                    f = c * per + 2 * i
                    multiply(f)
                    ring_copy(f, 0, 1).start()
                    multiply(f + 1)
                    ring_copy(f + 1, 0, -1).start()

            @pl.when(jnp.logical_and(t > 0, t < steps - 1))
            def _():
                @pl.loop(0, per // 2)
                def _(i):
                    for way in (1, -1):
                        f = c * per + 2 * i + (1 - way) // 2
                        goal, value = advance(f, t, way)
                        partial[f, goal] = value
                        ring_copy(f, t, way).start()

            @pl.when(t == steps - 1)
            def _():
                @pl.loop(0, per // 2)
                def _(i):
                    for way in (1, -1):
                        f = c * per + 2 * i + (1 - way) // 2
                        out[f] = advance(f, t, way)[1]

        for c in range(EARLY, CHUNKS):
            @pl.when(tick == c - EARLY)
            def _():
                spread(c)

    @pl.loop(0, CHUNKS)
    def _(c):
        @pl.loop(1, n_freq)
        def _(off):
            y_copy(c, off).wait_send()

        @pl.loop(1, n_apt)
        def _(off):
            z_copy(c, off).wait_send()

        @pl.loop(1, n_rcv)
        def _(off):
            x_copy(c, off).wait_send()

    @pl.loop(0, freqs)
    def _(f):
        @pl.loop(0, steps - 1)
        def _(t):
            ring_copy(f, t, 1).wait_send()


def on_device(sizes, shot_lists, block_ids, taper_ids, green_traces):
    n_freq, n_apt, n_rcv = sizes
    _, all_freqs, entries, parts, length = shot_lists.shape
    shots = block_ids.shape[0]
    freqs, _, points, width = green_traces.shape
    blocks = points // length
    lists = shot_lists.reshape(all_freqs, entries * parts, length)

    choose = (taper_ids[:, :, None] == jnp.arange(4, dtype=jnp.int32)).astype(jnp.float32)
    taper = jnp.sum(choose[:, :, :, None] * windows(length)[None, None, :, :], axis=2)
    taper = jnp.broadcast_to(taper[:, :, None, :], (shots, entries, parts, length))
    taper = taper.reshape(shots * entries * parts, length)

    rows, columns = n_apt * blocks * shots * parts, shots * entries * parts
    row, column = jnp.arange(rows)[:, None], jnp.arange(columns)[None, :]
    named = jnp.broadcast_to(block_ids[:, :, None], (shots, entries, parts)).reshape(1, columns)
    select = (
        (row // (shots * parts) == named)
        & (row // parts % shots == column // (entries * parts))
        & (row % parts == column % parts)
    ).astype(jnp.bfloat16)

    tile = shots * parts
    result = pl.pallas_call(
        functools.partial(kernel, sizes),
        out_shape=jax.ShapeDtypeStruct((freqs, n_rcv * tile, width), jnp.bfloat16),
        in_specs=[
            pl.BlockSpec(memory_space=pl.ANY),
            pl.BlockSpec(memory_space=pltpu.VMEM),
            pl.BlockSpec(memory_space=pltpu.VMEM),
            pl.BlockSpec(memory_space=pl.ANY),
        ],
        out_specs=pl.BlockSpec(memory_space=pltpu.VMEM),
        scratch_shapes=[
            pltpu.VMEM((shots, freqs, entries * parts, length), jnp.bfloat16),
            pltpu.VMEM((freqs, n_apt, blocks, tile, length), jnp.bfloat16),
            pltpu.VMEM((freqs, n_apt, n_rcv, blocks, tile, length), jnp.bfloat16),
            pltpu.VMEM((freqs, parts, points, width), jnp.bfloat16),
            pltpu.VMEM((freqs, n_apt, n_rcv * tile, width), jnp.bfloat16),
            pltpu.VMEM((freqs, n_apt - 1, n_rcv * tile, width), jnp.bfloat16),
            pltpu.SemaphoreType.DMA((freqs,)),
            pltpu.SemaphoreType.DMA((CHUNKS, n_freq)),
            pltpu.SemaphoreType.DMA((CHUNKS, n_freq)),
            pltpu.SemaphoreType.DMA((CHUNKS, n_apt)),
            pltpu.SemaphoreType.DMA((CHUNKS, n_apt)),
            pltpu.SemaphoreType.DMA((CHUNKS, n_rcv)),
            pltpu.SemaphoreType.DMA((CHUNKS, n_rcv)),
            pltpu.SemaphoreType.DMA((2, CHUNKS)),
            pltpu.SemaphoreType.DMA((freqs, n_apt - 1)),
            pltpu.SemaphoreType.DMA((freqs, n_apt - 1)),
        ],
        compiler_params=pltpu.CompilerParams(
            collective_id=0, has_side_effects=True, vmem_limit_bytes=52 * 1024 * 1024
        ),
    )(lists, taper, select, green_traces)
    return result.reshape(freqs, n_rcv * shots, parts, width).transpose(1, 0, 2, 3)


def solution(mesh):
    sizes = (mesh.shape["freq"], mesh.shape["apt"], mesh.shape["rcv"])
    return jax.shard_map(
        functools.partial(on_device, sizes),
        mesh=mesh,
        in_specs=(
            P(("apt", "rcv", "freq"), None, None, None, None),
            P(("apt", "rcv"), None),
            P(("apt", "rcv"), None),
            P("freq", None, "apt", "rcv"),
        ),
        out_specs=P("apt", "freq", None, "rcv"),
        check_vma=False,
    )
```

```python
import functools

import jax
import jax.numpy as jnp
from jax import lax
from jax.experimental import pallas as pl
from jax.experimental.pallas import tpu as pltpu
from jax.sharding import PartitionSpec as P

MESH = pl.DeviceIdType.MESH
CHUNKS = (2, 2, 2, 2, 4, 4)
PLAN = (
    "D0", "D1", "D2", "D4", "X0", "X1", "F0", "X2", "D3", "M0", "D5", "F1", "F2", "X3",
    "M1", "X4", "M2", "X5", "T", "F3", "T", "F4", "T", "F5", "M3", "T", "M6", "M7",
    "M4", "M5",
)


def windows(block_len):
    angles = jnp.pi * (jnp.arange(block_len, dtype=jnp.float32) + 0.5) / block_len
    cosine = jnp.cos(angles)
    return jnp.stack(
        [jnp.ones_like(cosine), 0.5 - 0.5 * cosine, 0.5 + 0.5 * cosine, jnp.sin(angles) ** 2],
        axis=0,
    )


def kernel(
    sizes,
    listed,
    ids,
    tapers,
    shape,
    green,
    out,
    named_ids,
    named_tapers,
    lists,
    raw,
    taper,
    select,
    dense,
    apert,
    held_green,
    partial,
    ring,
    load_sem,
    green_sem,
    own_sem,
    y_send,
    y_recv,
    z_send,
    z_recv,
    x_send,
    x_recv,
    ring_send,
    ring_recv,
):
    n_freq, n_apt, n_rcv = sizes
    me_f, me_z, me_x = lax.axis_index("freq"), lax.axis_index("apt"), lax.axis_index("rcv")
    freqs = held_green.shape[0]
    entries = named_ids.shape[1]
    last = n_apt - 1
    starts = [sum(CHUNKS[:c]) for c in range(len(CHUNKS))]

    loads = [
        pltpu.make_async_copy(source, target, load_sem.at[k])
        for k, (source, target) in enumerate(
            ((listed, lists), (ids, named_ids), (tapers, named_tapers))
        )
    ]
    for load in loads:
        load.start()

    barrier = pltpu.get_barrier_semaphore()
    for axis, me, size in (("freq", me_f, n_freq), ("apt", me_z, n_apt), ("rcv", me_x, n_rcv)):
        if axis == "rcv":
            offsets = (1, size - 1)
            for off in offsets:
                pl.semaphore_signal(
                    barrier, inc=1, device_id={axis: lax.rem(me + off, size)}, device_id_type=MESH
                )
        else:
            @pl.loop(1, size)
            def _(off):
                pl.semaphore_signal(
                    barrier, inc=1, device_id={axis: lax.rem(me + off, size)}, device_id_type=MESH
                )

    def span(c):
        return pl.ds(starts[c], CHUNKS[c])

    def own_lists(c):
        return pltpu.make_async_copy(
            lists.at[pl.ds(me_f * freqs + starts[c], CHUNKS[c])],
            raw.at[me_f, span(c)],
            own_sem.at[0, c],
        )

    def own_dense(c):
        return pltpu.make_async_copy(
            dense.at[span(c), me_z], apert.at[span(c), me_z, me_x], own_sem.at[1, c]
        )

    def green_copy(f):
        return pltpu.make_async_copy(green.at[f], held_green.at[f], green_sem.at[f])

    def y_copy(c, off):
        peer = lax.rem(me_f + off, n_freq)
        return pltpu.make_async_remote_copy(
            src_ref=lists.at[pl.ds(peer * freqs + starts[c], CHUNKS[c])],
            dst_ref=raw.at[me_f, span(c)],
            send_sem=y_send.at[c, off],
            recv_sem=y_recv.at[c, off],
            device_id={"freq": peer},
            device_id_type=MESH,
        )

    def z_copy(c, off):
        peer = lax.rem(me_z + off, n_apt)
        return pltpu.make_async_remote_copy(
            src_ref=dense.at[span(c), peer],
            dst_ref=apert.at[span(c), me_z, me_x],
            send_sem=z_send.at[c, off],
            recv_sem=z_recv.at[c, off],
            device_id={"apt": peer},
            device_id_type=MESH,
        )

    def x_copy(c, kind):
        way = (1, -1)[kind % 2]
        if kind < 2:
            block = apert.at[span(c), :, me_x]
        else:
            part = CHUNKS[c] // 2
            which = pl.ds(starts[c] + (part if way < 0 else 0), part)
            block = apert.at[which, :, lax.rem(me_x - way + n_rcv, n_rcv)]
        return pltpu.make_async_remote_copy(
            src_ref=block,
            dst_ref=block,
            send_sem=x_send.at[c, kind],
            recv_sem=x_recv.at[c, kind],
            device_id={"rcv": lax.rem(me_x + way + n_rcv, n_rcv)},
            device_id_type=MESH,
        )

    def goal_of(t, way):
        return lax.rem(me_z - way * (1 + t) + 2 * n_apt, n_apt)

    def ring_copy(p, t, way):
        turn = (1 - way) // 2
        return pltpu.make_async_remote_copy(
            src_ref=partial.at[2 * p + turn, goal_of(t, way)],
            dst_ref=ring.at[t, 2 * p + turn],
            send_sem=ring_send.at[p, t, turn],
            recv_sem=ring_recv.at[p, t, turn],
            device_id={"apt": lax.rem(me_z + way + n_apt, n_apt)},
            device_id_type=MESH,
        )

    loads[0].wait()
    pl.semaphore_wait(barrier, n_freq + n_apt)
    for c in range(len(CHUNKS)):
        @pl.loop(1, n_freq)
        def _(off):
            y_copy(c, off).start()

        own_lists(c).start()

    @pl.loop(0, freqs)
    def _(f):
        green_copy(f).start()

    loads[1].wait()
    loads[2].wait()
    rows, columns = select.shape
    tile = 2 * n_freq
    row = lax.broadcasted_iota(jnp.int32, (rows, columns), 0)
    column = lax.broadcasted_iota(jnp.int32, (8, columns), 1)
    strip_row = lax.broadcasted_iota(jnp.int32, taper.shape, 0) // 2
    named = jnp.zeros((8, columns), jnp.int32)
    chosen = jnp.zeros(taper.shape, jnp.int32)
    for k in range(n_freq * entries):
        named = jnp.where(column // 2 == k, named_ids[k // entries, k % entries], named)
        chosen = jnp.where(strip_row == k, named_tapers[k // entries, k % entries], chosen)
    goal_row = named * tile + column // (2 * entries) * 2 + column % 2
    hit = row == jnp.broadcast_to(goal_row[0:1], (rows, columns))
    select[...] = jnp.where(hit, 1.0, 0.0).astype(jnp.bfloat16)
    weights = jnp.broadcast_to(shape[0:1, :], taper.shape)
    for w in range(1, 4):
        weights = jnp.where(chosen == w, jnp.broadcast_to(shape[w : w + 1, :], taper.shape), weights)
    taper[...] = weights

    def place(c):
        own_lists(c).wait()

        @pl.loop(1, n_freq)
        def _(off):
            y_copy(c, off).wait_recv()

        @pl.loop(0, CHUNKS[c])
        def _(i):
            f = starts[c] + i
            weighed = raw[:, f].reshape(taper.shape).astype(jnp.float32) * taper[...]
            placed = jnp.dot(
                select[...], weighed.astype(jnp.bfloat16), preferred_element_type=jnp.float32
            )
            dense[f] = placed.astype(jnp.bfloat16).reshape(dense.shape[1:])

        @pl.loop(1, n_apt)
        def _(off):
            z_copy(c, off).start()

        own_dense(c).start()

    def spread(c):
        own_dense(c).wait()

        @pl.loop(1, n_apt)
        def _(off):
            z_copy(c, off).wait_recv()

        x_copy(c, 0).start()
        x_copy(c, 1).start()

    def forward(c):
        x_copy(c, 0).wait_recv()
        x_copy(c, 2).start()
        x_copy(c, 1).wait_recv()
        x_copy(c, 3).start()

    gathered = set()

    def multiply(p):
        c = max(k for k, start in enumerate(starts) if start <= 2 * p)
        if c not in gathered:
            gathered.add(c)
            x_copy(c, 2).wait_recv()
            x_copy(c, 3).wait_recv()
        blocks, depth = apert.shape[3], apert.shape[5]
        count = n_apt * n_rcv * tile
        for way in (1, -1):
            f = 2 * p + (1 - way) // 2
            green_copy(f).wait()
            left = jnp.concatenate(
                [apert[f, :, :, b].reshape(count, depth) for b in range(blocks)], axis=1
            )
            wide = left.astype(jnp.float32).reshape(count // 8, 8, blocks * depth)
            odd = lax.rem(lax.broadcasted_iota(jnp.int32, wide.shape, 1), 2) == 1
            turned = jnp.where(odd, pltpu.roll(wide, 1, 1), -pltpu.roll(wide, 7, 1))
            turned = turned.reshape(count, blocks * depth).astype(jnp.bfloat16)
            both = jnp.concatenate([left, turned], axis=1)
            right = held_green[f].reshape(2 * held_green.shape[2], held_green.shape[3])
            sums = jnp.dot(both, right, preferred_element_type=jnp.float32)
            partial[f] = sums.astype(jnp.bfloat16).reshape(partial.shape[1:])
            ring_copy(p, 0, way).start()

    def advance(p, t):
        for way in (1, -1):
            f = 2 * p + (1 - way) // 2
            ring_copy(p, t - 1, way).wait_recv()
            goal = goal_of(t, way)
            value = ring[t - 1, f] + partial[f, goal]
            if t < last:
                partial[f, goal] = value
                ring_copy(p, t, way).start()
            else:
                out[f] = value

    going = {}

    def tick():
        for p in list(going):
            going[p] += 1
            advance(p, going[p])
            if going[p] == last:
                del going[p]

    for event in PLAN:
        if event == "T":
            tick()
        else:
            {"D": place, "X": spread, "F": forward, "M": multiply}[event[0]](int(event[1]))
            if event[0] == "M":
                going[int(event[1])] = 0
    while going:
        tick()

    for c in range(len(CHUNKS)):
        @pl.loop(1, n_freq)
        def _(off):
            y_copy(c, off).wait_send()

        @pl.loop(1, n_apt)
        def _(off):
            z_copy(c, off).wait_send()

        for kind in range(4):
            x_copy(c, kind).wait_send()

    @pl.loop(0, freqs // 2)
    def _(p):
        @pl.loop(0, last)
        def _(t):
            for way in (1, -1):
                ring_copy(p, t, way).wait_send()


def on_device(sizes, shot_lists, block_ids, taper_ids, green_traces):
    n_freq, n_apt, n_rcv = sizes
    _, all_freqs, entries, parts, length = shot_lists.shape
    shots = block_ids.shape[0]
    freqs, _, points, width = green_traces.shape
    blocks = points // length
    lists = shot_lists.reshape(all_freqs, entries * parts, length)
    tile = shots * parts
    chunks = len(CHUNKS)
    dma = pltpu.SemaphoreType.DMA
    result = pl.pallas_call(
        functools.partial(kernel, sizes),
        out_shape=jax.ShapeDtypeStruct((freqs, n_rcv * tile, width), jnp.bfloat16),
        in_specs=[
            pl.BlockSpec(memory_space=pl.ANY),
            pl.BlockSpec(memory_space=pl.ANY),
            pl.BlockSpec(memory_space=pl.ANY),
            pl.BlockSpec(memory_space=pltpu.VMEM),
            pl.BlockSpec(memory_space=pl.ANY),
        ],
        out_specs=pl.BlockSpec(memory_space=pltpu.VMEM),
        scratch_shapes=[
            pltpu.SMEM(block_ids.shape, jnp.int32),
            pltpu.SMEM(taper_ids.shape, jnp.int32),
            pltpu.VMEM(lists.shape, jnp.bfloat16),
            pltpu.VMEM((shots, freqs, entries * parts, length), jnp.bfloat16),
            pltpu.VMEM((shots * entries * parts, length), jnp.float32),
            pltpu.VMEM((n_apt * blocks * tile, shots * entries * parts), jnp.bfloat16),
            pltpu.VMEM((freqs, n_apt, blocks, tile, length), jnp.bfloat16),
            pltpu.VMEM((freqs, n_apt, n_rcv, blocks, tile, length), jnp.bfloat16),
            pltpu.VMEM((freqs, parts, points, width), jnp.bfloat16),
            pltpu.VMEM((freqs, n_apt, n_rcv * tile, width), jnp.bfloat16),
            pltpu.VMEM((n_apt - 1, freqs, n_rcv * tile, width), jnp.bfloat16),
            dma((3,)),
            dma((freqs,)),
            dma((2, chunks)),
            dma((chunks, n_freq)),
            dma((chunks, n_freq)),
            dma((chunks, n_apt)),
            dma((chunks, n_apt)),
            dma((chunks, 4)),
            dma((chunks, 4)),
            dma((freqs // 2, n_apt - 1, 2)),
            dma((freqs // 2, n_apt - 1, 2)),
        ],
        compiler_params=pltpu.CompilerParams(
            collective_id=0, has_side_effects=True, vmem_limit_bytes=56 * 1024 * 1024
        ),
    )(lists, block_ids, taper_ids, windows(length), green_traces)
    return result.reshape(freqs, n_rcv * shots, parts, width).transpose(1, 0, 2, 3)


def solution(mesh):
    sizes = (mesh.shape["freq"], mesh.shape["apt"], mesh.shape["rcv"])
    return jax.shard_map(
        functools.partial(on_device, sizes),
        mesh=mesh,
        in_specs=(
            P(("apt", "rcv", "freq"), None, None, None, None),
            P(("apt", "rcv"), None),
            P(("apt", "rcv"), None),
            P("freq", None, "apt", "rcv"),
        ),
        out_specs=P("apt", "freq", None, "rcv"),
        check_vma=False,
    )
```

```python
import functools

import jax
import jax.numpy as jnp
from jax import lax
from jax.experimental import pallas as pl
from jax.experimental.pallas import tpu as pltpu
from jax.sharding import PartitionSpec as P

MESH = pl.DeviceIdType.MESH
CHUNKS = (2, 2, 2, 2, 4, 4)
PLAN = (
    "D0", "D1", "D2", "D4", "X0", "X1", "F0", "X2", "D3", "M0", "D5", "F1", "F2", "X3",
    "M1", "X4", "M2", "X5", "T", "F3", "T", "F4", "T", "F5", "M3", "T", "M6", "M7",
    "M4", "M5",
)


def windows(block_len):
    angles = jnp.pi * (jnp.arange(block_len, dtype=jnp.float32) + 0.5) / block_len
    cosine = jnp.cos(angles)
    return jnp.stack(
        [jnp.ones_like(cosine), 0.5 - 0.5 * cosine, 0.5 + 0.5 * cosine, jnp.sin(angles) ** 2],
        axis=0,
    )


def kernel(
    sizes,
    listed,
    ids,
    tapers,
    shape,
    green,
    out,
    named_ids,
    named_tapers,
    lists,
    raw,
    taper,
    select,
    dense,
    apert,
    held_green,
    partial,
    ring,
    load_sem,
    green_sem,
    own_sem,
    y_send,
    y_recv,
    z_send,
    z_recv,
    x_send,
    x_recv,
    ring_send,
    ring_recv,
):
    n_freq, n_apt, n_rcv = sizes
    me_f, me_z, me_x = lax.axis_index("freq"), lax.axis_index("apt"), lax.axis_index("rcv")
    freqs = held_green.shape[0]
    entries = named_ids.shape[1]
    last = n_apt - 1
    starts = [sum(CHUNKS[:c]) for c in range(len(CHUNKS))]

    loads = [
        pltpu.make_async_copy(source, target, load_sem.at[k])
        for k, (source, target) in enumerate(
            ((listed, lists), (ids, named_ids), (tapers, named_tapers))
        )
    ]
    for load in loads:
        load.start()

    barrier = pltpu.get_barrier_semaphore()
    for axis, me, size in (("freq", me_f, n_freq), ("apt", me_z, n_apt), ("rcv", me_x, n_rcv)):
        if axis == "rcv":
            offsets = (1, size - 1)
            for off in offsets:
                pl.semaphore_signal(
                    barrier, inc=1, device_id={axis: lax.rem(me + off, size)}, device_id_type=MESH
                )
        else:
            @pl.loop(1, size)
            def _(off):
                pl.semaphore_signal(
                    barrier, inc=1, device_id={axis: lax.rem(me + off, size)}, device_id_type=MESH
                )

    def span(c):
        return pl.ds(starts[c], CHUNKS[c])

    def own_lists(c):
        return pltpu.make_async_copy(
            lists.at[pl.ds(me_f * freqs + starts[c], CHUNKS[c])],
            raw.at[me_f, span(c)],
            own_sem.at[0, c],
        )

    def own_dense(c):
        return pltpu.make_async_copy(
            dense.at[span(c), me_z], apert.at[span(c), me_z, me_x], own_sem.at[1, c]
        )

    def green_copy(f):
        return pltpu.make_async_copy(green.at[f], held_green.at[f], green_sem.at[f])

    def y_copy(c, off):
        peer = lax.rem(me_f + off, n_freq)
        return pltpu.make_async_remote_copy(
            src_ref=lists.at[pl.ds(peer * freqs + starts[c], CHUNKS[c])],
            dst_ref=raw.at[me_f, span(c)],
            send_sem=y_send.at[c, off],
            recv_sem=y_recv.at[c, off],
            device_id={"freq": peer},
            device_id_type=MESH,
        )

    def z_copy(c, off):
        peer = lax.rem(me_z + off, n_apt)
        return pltpu.make_async_remote_copy(
            src_ref=dense.at[span(c), peer],
            dst_ref=apert.at[span(c), me_z, me_x],
            send_sem=z_send.at[c, off],
            recv_sem=z_recv.at[c, off],
            device_id={"apt": peer},
            device_id_type=MESH,
        )

    def x_copy(c, kind):
        way = (1, -1)[kind % 2]
        if kind < 2:
            block = apert.at[span(c), :, me_x]
        else:
            part = CHUNKS[c] // 2
            which = pl.ds(starts[c] + (part if way < 0 else 0), part)
            block = apert.at[which, :, lax.rem(me_x - way + n_rcv, n_rcv)]
        return pltpu.make_async_remote_copy(
            src_ref=block,
            dst_ref=block,
            send_sem=x_send.at[c, kind],
            recv_sem=x_recv.at[c, kind],
            device_id={"rcv": lax.rem(me_x + way + n_rcv, n_rcv)},
            device_id_type=MESH,
        )

    def goal_of(t, way):
        return lax.rem(me_z - way * (1 + t) + 2 * n_apt, n_apt)

    def ring_copy(p, t, way):
        turn = (1 - way) // 2
        return pltpu.make_async_remote_copy(
            src_ref=partial.at[2 * p + turn, goal_of(t, way)],
            dst_ref=ring.at[t, 2 * p + turn],
            send_sem=ring_send.at[p, t, turn],
            recv_sem=ring_recv.at[p, t, turn],
            device_id={"apt": lax.rem(me_z + way + n_apt, n_apt)},
            device_id_type=MESH,
        )

    loads[0].wait()
    pl.semaphore_wait(barrier, n_freq + n_apt)
    for c in range(len(CHUNKS)):
        @pl.loop(1, n_freq)
        def _(off):
            y_copy(c, off).start()

        own_lists(c).start()

    @pl.loop(0, freqs)
    def _(f):
        green_copy(f).start()

    loads[1].wait()
    loads[2].wait()
    rows, columns = select.shape
    tile = 2 * n_freq
    row = lax.broadcasted_iota(jnp.int32, (rows, columns), 0)
    column = lax.broadcasted_iota(jnp.int32, (8, columns), 1)
    strip_row = lax.broadcasted_iota(jnp.int32, taper.shape, 0) // 2
    named = jnp.zeros((8, columns), jnp.int32)
    chosen = jnp.zeros(taper.shape, jnp.int32)
    for k in range(n_freq * entries):
        named = jnp.where(column // 2 == k, named_ids[k // entries, k % entries], named)
        chosen = jnp.where(strip_row == k, named_tapers[k // entries, k % entries], chosen)
    goal_row = named * tile + column // (2 * entries) * 2 + column % 2
    hit = row == jnp.broadcast_to(goal_row[0:1], (rows, columns))
    select[...] = jnp.where(hit, 1.0, 0.0).astype(jnp.bfloat16)
    weights = jnp.broadcast_to(shape[0:1, :], taper.shape)
    for w in range(1, 4):
        weights = jnp.where(chosen == w, jnp.broadcast_to(shape[w : w + 1, :], taper.shape), weights)
    taper[...] = weights

    def place(c):
        own_lists(c).wait()

        @pl.loop(1, n_freq)
        def _(off):
            y_copy(c, off).wait_recv()

        @pl.loop(0, CHUNKS[c])
        def _(i):
            f = starts[c] + i
            weighed = raw[:, f].reshape(taper.shape).astype(jnp.float32) * taper[...]
            placed = jnp.dot(
                select[...], weighed.astype(jnp.bfloat16), preferred_element_type=jnp.float32
            )
            dense[f] = placed.astype(jnp.bfloat16).reshape(dense.shape[1:])

        @pl.loop(1, n_apt)
        def _(off):
            z_copy(c, off).start()

        own_dense(c).start()

    def spread(c):
        own_dense(c).wait()

        @pl.loop(1, n_apt)
        def _(off):
            z_copy(c, off).wait_recv()

        x_copy(c, 0).start()
        x_copy(c, 1).start()

    def forward(c):
        x_copy(c, 0).wait_recv()
        x_copy(c, 2).start()
        x_copy(c, 1).wait_recv()
        x_copy(c, 3).start()

    gathered = set()

    def multiply(p):
        c = max(k for k, start in enumerate(starts) if start <= 2 * p)
        if c not in gathered:
            gathered.add(c)
            x_copy(c, 2).wait_recv()
            x_copy(c, 3).wait_recv()
        blocks, depth = apert.shape[3], apert.shape[5]
        count = n_apt * n_rcv * tile
        for way in (1, -1):
            f = 2 * p + (1 - way) // 2
            green_copy(f).wait()
            left = jnp.concatenate(
                [apert[f, :, :, b].reshape(count, depth) for b in range(blocks)], axis=1
            )
            wide = left.astype(jnp.float32).reshape(count // 8, 8, blocks * depth)
            odd = lax.rem(lax.broadcasted_iota(jnp.int32, wide.shape, 1), 2) == 1
            turned = jnp.where(odd, pltpu.roll(wide, 1, 1), -pltpu.roll(wide, 7, 1))
            turned = turned.reshape(count, blocks * depth).astype(jnp.bfloat16)
            both = jnp.concatenate([left, turned], axis=1)
            right = held_green[f].reshape(2 * held_green.shape[2], held_green.shape[3])
            sums = jnp.dot(both, right, preferred_element_type=jnp.float32)
            partial[f] = sums.astype(jnp.bfloat16).reshape(partial.shape[1:])
            ring_copy(p, 0, way).start()

    def advance(p, t):
        for way in (1, -1):
            f = 2 * p + (1 - way) // 2
            ring_copy(p, t - 1, way).wait_recv()
            goal = goal_of(t, way)
            value = ring[t - 1, f] + partial[f, goal]
            if t < last:
                partial[f, goal] = value
                ring_copy(p, t, way).start()
            else:
                for k in range(out.shape[1]):
                    out[f, k] = value[:, k * out.shape[3] : (k + 1) * out.shape[3]]

    going = {}

    def tick():
        for p in list(going):
            going[p] += 1
            advance(p, going[p])
            if going[p] == last:
                del going[p]

    for event in PLAN:
        if event == "T":
            tick()
        else:
            {"D": place, "X": spread, "F": forward, "M": multiply}[event[0]](int(event[1]))
            if event[0] == "M":
                going[int(event[1])] = 0
    while going:
        tick()

    for c in range(len(CHUNKS)):
        @pl.loop(1, n_freq)
        def _(off):
            y_copy(c, off).wait_send()

        @pl.loop(1, n_apt)
        def _(off):
            z_copy(c, off).wait_send()

        for kind in range(4):
            x_copy(c, kind).wait_send()

    @pl.loop(0, freqs // 2)
    def _(p):
        @pl.loop(0, last)
        def _(t):
            for way in (1, -1):
                ring_copy(p, t, way).wait_send()


def on_device(sizes, shot_lists, block_ids, taper_ids, green_traces):
    n_freq, n_apt, n_rcv = sizes
    _, all_freqs, entries, parts, length = shot_lists.shape
    shots = block_ids.shape[0]
    freqs, _, points, width = green_traces.shape
    blocks = points // length
    lists = shot_lists.reshape(all_freqs, entries * parts, length)
    tile = shots * parts
    chunks = len(CHUNKS)
    dma = pltpu.SemaphoreType.DMA
    result = pl.pallas_call(
        functools.partial(kernel, sizes),
        out_shape=jax.ShapeDtypeStruct((freqs, width // length, n_rcv * tile, length), jnp.bfloat16),
        in_specs=[
            pl.BlockSpec(memory_space=pl.ANY),
            pl.BlockSpec(memory_space=pl.ANY),
            pl.BlockSpec(memory_space=pl.ANY),
            pl.BlockSpec(memory_space=pltpu.VMEM),
            pl.BlockSpec(memory_space=pl.ANY),
        ],
        out_specs=pl.BlockSpec(memory_space=pltpu.VMEM),
        scratch_shapes=[
            pltpu.SMEM(block_ids.shape, jnp.int32),
            pltpu.SMEM(taper_ids.shape, jnp.int32),
            pltpu.VMEM(lists.shape, jnp.bfloat16),
            pltpu.VMEM((shots, freqs, entries * parts, length), jnp.bfloat16),
            pltpu.VMEM((shots * entries * parts, length), jnp.float32),
            pltpu.VMEM((n_apt * blocks * tile, shots * entries * parts), jnp.bfloat16),
            pltpu.VMEM((freqs, n_apt, blocks, tile, length), jnp.bfloat16),
            pltpu.VMEM((freqs, n_apt, n_rcv, blocks, tile, length), jnp.bfloat16),
            pltpu.VMEM((freqs, parts, points, width), jnp.bfloat16),
            pltpu.VMEM((freqs, n_apt, n_rcv * tile, width), jnp.bfloat16),
            pltpu.VMEM((n_apt - 1, freqs, n_rcv * tile, width), jnp.bfloat16),
            dma((3,)),
            dma((freqs,)),
            dma((2, chunks)),
            dma((chunks, n_freq)),
            dma((chunks, n_freq)),
            dma((chunks, n_apt)),
            dma((chunks, n_apt)),
            dma((chunks, 4)),
            dma((chunks, 4)),
            dma((freqs // 2, n_apt - 1, 2)),
            dma((freqs // 2, n_apt - 1, 2)),
        ],
        compiler_params=pltpu.CompilerParams(
            collective_id=0, has_side_effects=True, vmem_limit_bytes=56 * 1024 * 1024
        ),
    )(lists, block_ids, taper_ids, windows(length), green_traces)
    result = result.reshape(freqs, width // length, n_rcv * shots, parts, length)
    return result.transpose(2, 0, 3, 1, 4).reshape(n_rcv * shots, freqs, parts, width)


def solution(mesh):
    sizes = (mesh.shape["freq"], mesh.shape["apt"], mesh.shape["rcv"])
    return jax.shard_map(
        functools.partial(on_device, sizes),
        mesh=mesh,
        in_specs=(
            P(("apt", "rcv", "freq"), None, None, None, None),
            P(("apt", "rcv"), None),
            P(("apt", "rcv"), None),
            P("freq", None, "apt", "rcv"),
        ),
        out_specs=P("apt", "freq", None, "rcv"),
        check_vma=False,
    )
```
